32 devices in a mesh: tensor: 4 (over z), seq: 8 (over y, x, core).
Axes of the slice: x: 2, y: 2, z: 4, core: 2. Of those that a mesh axis runs over, the one named last changes fastest.
Arguments:
- teacher_q: bfloat16 [4096, 8192], P('seq', 'tensor'), may hold values from -24 to 24
- teacher_v: bfloat16 [4096, 8192], P('seq', 'tensor'), may hold values from -24 to 24
- student_q: bfloat16 [4096, 2048], P('seq'), may hold values from -24 to 24
- student_v: bfloat16 [4096, 2048], P('seq'), may hold values from -24 to 24
Outputs:
- grad_q: bfloat16 [4096, 2048], P('seq')
- grad_v: bfloat16 [4096, 2048], P('seq')
The draws below stay inside these ranges and needn't reach their ends.
All inputs are finite; a program needn't handle non-finite values.
Results may differ from the reference program's by a relative error of at most 0.0095.
Values may be sent and summed in bfloat16 or wider, within the bound.
A program may use at most 128 MiB of HBM per device.

```python
import jax
import jax.numpy as jnp
from jax import lax

DT = 8192
DS = 2048
HEADS = 32
SEQS = 2
TDH = 256
SDH = 64
TOKENS = 4096
LEN = 2048


def relation_rows(key, row_count, width, scale):
    subkeys = jax.random.split(key, 1)
    drawn = jnp.clip(jax.random.normal(subkeys[0], (row_count, width), jnp.float32), -6.0, 6.0) * scale
    return drawn.astype(jnp.bfloat16)


def draw_teacher_q(key, part):
    return relation_rows(jax.random.fold_in(key, 11), TOKENS, DT, 0.6)


def draw_teacher_v(key, part):
    return relation_rows(jax.random.fold_in(key, 23), TOKENS, DT, 0.6)


def draw_student_q(key, part):
    return relation_rows(jax.random.fold_in(key, 37), TOKENS, DS, 0.85)


def draw_student_v(key, part):
    return relation_rows(jax.random.fold_in(key, 41), TOKENS, DS, 0.85)


def setup_inputs(seed: int = 0) -> dict:
    arg_keys = jax.random.split(jax.random.key(seed), 5)
    teacher_q = draw_teacher_q(jax.random.fold_in(arg_keys[4], 71), 0)
    teacher_v = draw_teacher_v(jax.random.fold_in(arg_keys[4], 71), 0)
    student_q = draw_student_q(jax.random.fold_in(arg_keys[4], 71), 0)
    student_v = draw_student_v(jax.random.fold_in(arg_keys[4], 71), 0)
    return dict(teacher_q=teacher_q, teacher_v=teacher_v, student_q=student_q, student_v=student_v)


def head_grad(pair):
    teach_head, stud_head = pair
    teach_scores = jnp.dot(teach_head, teach_head.T, preferred_element_type=jnp.float32) * TDH ** (-0.5)
    stud_scores = jnp.dot(stud_head, stud_head.T, preferred_element_type=jnp.float32) * SDH ** (-0.5)
    teach_prob = jax.nn.softmax(teach_scores, axis=-1)
    stud_prob = jax.nn.softmax(stud_scores, axis=-1)
    coef = (256.0 * SDH ** (-0.5) * (stud_prob - teach_prob)).astype(jnp.bfloat16).astype(jnp.float32)
    return jnp.dot(coef, stud_head, preferred_element_type=jnp.float32) + jnp.dot(coef.T, stud_head, preferred_element_type=jnp.float32)

def relation_grad(teacher, student):
    pieces = []
    for seq_num in range(SEQS):
        teach_rows = teacher[seq_num * LEN:(seq_num + 1) * LEN].astype(jnp.float32)
        stud_rows = student[seq_num * LEN:(seq_num + 1) * LEN].astype(jnp.float32)
        teach_heads = teach_rows.reshape(LEN, HEADS, TDH).transpose(1, 0, 2)
        stud_heads = stud_rows.reshape(LEN, HEADS, SDH).transpose(1, 0, 2)
        grads = lax.map(head_grad, (teach_heads, stud_heads))
        pieces.append(grads.transpose(1, 0, 2).reshape(LEN, DS))
    return jnp.concatenate(pieces, axis=0).astype(jnp.bfloat16)

def reference(teacher_q, teacher_v, student_q, student_v):
    return (relation_grad(teacher_q, student_q), relation_grad(teacher_v, student_v))
```

```python
import functools
import math

import jax
import jax.numpy as jnp
from jax import lax
from jax.experimental import pallas as pl
from jax.experimental.pallas import tpu as pltpu
from jax.sharding import PartitionSpec as P

HEADS = 32
SEQS = 2
BLOCK = 256
LOG2E = math.log2(math.e)


def softmax_terms(scores, scale):
    scaled = scores * (scale * LOG2E)
    shifted = jnp.exp2(scaled - jnp.max(scaled, axis=0, keepdims=True))
    return shifted, jnp.sum(shifted, axis=0, keepdims=True)


def pair_block(teach, stud, stud_t, grad, start, tdh, sdh):
    rows = pl.ds(start, BLOCK)
    stud_own = stud[rows, :]
    lane = lax.broadcasted_iota(jnp.int32, stud_own.shape, 1)
    key_side = None
    query_side = []
    for head in range(2):
        columns = slice(head * tdh, (head + 1) * tdh)
        masked = jnp.where(lane // sdh == head, stud_own, jnp.zeros_like(stud_own))
        dims = (((1,), (1,)), ((), ()))
        teach_scores = lax.dot_general(teach[:, columns], teach[rows, columns], dims, preferred_element_type=jnp.float32)
        stud_scores = lax.dot_general(stud[...], masked, dims, preferred_element_type=jnp.float32)
        teach_exp, teach_sum = softmax_terms(teach_scores, tdh**-0.5)
        stud_exp, stud_sum = softmax_terms(stud_scores, sdh**-0.5)
        factor = 256.0 * sdh**-0.5
        coef = (stud_exp * (factor / stud_sum) - teach_exp * (factor / teach_sum)).astype(jnp.bfloat16)
        part = jnp.dot(coef, masked, preferred_element_type=jnp.float32)
        key_side = part if key_side is None else key_side + part
        query_side.append(
            jnp.dot(stud_t[head * sdh : (head + 1) * sdh, :], coef, preferred_element_type=jnp.float32)
        )
    grad[...] += key_side
    grad[rows, :] += jnp.concatenate(query_side, axis=0).T


def pair_kernel(tdh, sdh, teach, stud, out, stud_t, grad):
    length = teach.shape[0]
    stud_t[...] = stud[...].T
    grad[...] = jnp.zeros_like(grad)

    @pl.loop(0, length // BLOCK)
    def _(block):
        pair_block(teach, stud, stud_t, grad, pl.multiple_of(block * BLOCK, BLOCK), tdh, sdh)

    out[...] = grad[...].astype(out.dtype)


def pair_grad(teach, stud, tdh, sdh):
    length = teach.shape[0]
    return pl.pallas_call(
        functools.partial(pair_kernel, tdh, sdh),
        out_shape=jax.ShapeDtypeStruct((length, 2 * sdh), jnp.bfloat16),
        in_specs=[pl.BlockSpec(memory_space=pltpu.VMEM)] * 2,
        out_specs=pl.BlockSpec(memory_space=pltpu.VMEM),
        scratch_shapes=[
            pltpu.VMEM((2 * sdh, length), jnp.bfloat16),
            pltpu.VMEM((length, 2 * sdh), jnp.float32),
        ],
        compiler_params=pltpu.CompilerParams(vmem_limit_bytes=56 * 2**20),
    )(teach, stud)


def shards_pairs(teacher_q, teacher_v, student_q, student_v):
    n_tensor = lax.axis_size("tensor")
    n_seq = lax.axis_size("seq")
    group_size = n_seq // SEQS
    groups = [[s * group_size + m for m in range(group_size)] for s in range(SEQS)]
    per_dev = HEADS // n_tensor
    tdh = teacher_q.shape[1] // per_dev
    sdh = student_q.shape[1] // HEADS
    own_width = per_dev * sdh
    offset = lax.axis_index("tensor") * own_width

    def exchange(array, split_axis, concat_axis):
        return lax.all_to_all(
            array, "seq", split_axis, concat_axis, tiled=True, axis_index_groups=groups
        )

    def relation(teacher, student):
        teach = exchange(teacher, 1, 0)
        stud = exchange(lax.dynamic_slice_in_dim(student, offset, own_width, 1), 1, 0)
        grad = pair_grad(teach, stud, tdh, sdh)
        return lax.all_gather(exchange(grad, 0, 1), "tensor", axis=1, tiled=True)

    return (relation(teacher_q, student_q), relation(teacher_v, student_v))


def from_partner(array, axis, distance):
    return lax.ppermute(array, axis, [(i, i ^ 1 << distance) for i in range(lax.axis_size(axis))])


def head_terms(teach_query, teach_key, stud_query, stud_key, teach_dim, stud_dim):
    teach_scores = jnp.dot(
        teach_query, teach_key.T, preferred_element_type=jnp.float32
    ) * teach_dim ** (-0.5)
    stud_scores = jnp.dot(
        stud_query, stud_key.T, preferred_element_type=jnp.float32
    ) * stud_dim ** (-0.5)
    teach_prob = jax.nn.softmax(teach_scores, axis=-1)
    stud_prob = jax.nn.softmax(stud_scores, axis=-1)
    coef = (256.0 * stud_dim ** (-0.5) * (stud_prob - teach_prob)).astype(jnp.bfloat16)
    query_grad = jnp.dot(coef, stud_key, preferred_element_type=jnp.float32)
    key_grad = jnp.einsum("qk,qd->kd", coef, stud_query, preferred_element_type=jnp.float32)
    return (query_grad, key_grad)


def relate(teach_own, teach_keys, stud_own, stud_keys, per_dev, teach_dim, stud_dim):
    tok_rows = teach_own.shape[0]
    teach_query = teach_own.reshape(tok_rows, per_dev, teach_dim).transpose(1, 0, 2)
    teach_key = teach_keys.reshape(-1, per_dev, teach_dim).transpose(1, 0, 2)
    stud_query = stud_own.reshape(tok_rows, per_dev, stud_dim).transpose(1, 0, 2)
    stud_key = stud_keys.reshape(-1, per_dev, stud_dim).transpose(1, 0, 2)

    def one_head(group):
        return head_terms(group[0], group[1], group[2], group[3], teach_dim, stud_dim)

    query_grad, key_grad = lax.map(one_head, (teach_query, teach_key, stud_query, stud_key))
    return (
        query_grad.transpose(1, 0, 2).reshape(tok_rows, per_dev * stud_dim),
        key_grad.transpose(1, 0, 2).reshape(-1, per_dev * stud_dim),
    )


def shards(teacher_q, teacher_v, student_q, student_v):
    n_tensor = lax.axis_size("tensor")
    n_seq = lax.axis_size("seq")
    per_dev = HEADS // n_tensor
    group_size = n_seq // SEQS
    level_count = group_size.bit_length() - 1
    seq_index = lax.axis_index("seq")
    member = seq_index % group_size
    teach_dim = teacher_q.shape[1] // per_dev
    stud_dim = student_q.shape[1] // HEADS
    own_width = per_dev * stud_dim
    offset = lax.axis_index("tensor") * own_width
    own_q = lax.dynamic_slice_in_dim(student_q, offset, own_width, 1)
    own_v = lax.dynamic_slice_in_dim(student_v, offset, own_width, 1)
    key_tq, key_tv, key_sq, key_sv = (teacher_q, teacher_v, own_q, own_v)
    for bit_num in range(level_count):
        partner = from_partner((key_tq, key_tv, key_sq, key_sv), "seq", bit_num)
        upper_half = member // 2**bit_num % 2 == 1
        joined = []
        for mine, theirs in zip((key_tq, key_tv, key_sq, key_sv), partner):
            joined.append(
                jnp.where(
                    upper_half,
                    jnp.concatenate([theirs, mine], 0),
                    jnp.concatenate([mine, theirs], 0),
                )
            )
        key_tq, key_tv, key_sq, key_sv = joined
    q_query, q_key = relate(teacher_q, key_tq, own_q, key_sq, per_dev, teach_dim, stud_dim)
    v_query, v_key = relate(teacher_v, key_tv, own_v, key_sv, per_dev, teach_dim, stud_dim)
    returned = jnp.concatenate([q_key, v_key], axis=1)
    for bit_num in reversed(range(level_count)):
        half_rows = returned.shape[0] // 2
        upper_half = member // 2**bit_num % 2 == 1
        low_part = returned[:half_rows]
        high_part = returned[half_rows:]
        kept = jnp.where(upper_half, high_part, low_part)
        outgoing = jnp.where(upper_half, low_part, high_part)
        returned = kept + from_partner(outgoing.astype(jnp.bfloat16), "seq", bit_num).astype(
            outgoing.dtype
        )
    head_q = (q_query + returned[:, :own_width]).astype(jnp.bfloat16)
    head_v = (v_query + returned[:, own_width:]).astype(jnp.bfloat16)
    full_q, full_v = (
        lax.all_gather(head_q, "tensor", axis=1, tiled=True),
        lax.all_gather(head_v, "tensor", axis=1, tiled=True),
    )
    return (full_q, full_v)


def solution(mesh):
    per_dev = HEADS // mesh.shape["tensor"]
    group_size = mesh.shape["seq"] // SEQS
    body = shards_pairs if per_dev == 2 * group_size else shards
    in_specs = (P("seq", "tensor"), P("seq", "tensor"), P("seq", None), P("seq", None))
    out_specs = (P("seq", None), P("seq", None))
    return jax.shard_map(body, mesh=mesh, in_specs=in_specs, out_specs=out_specs, check_vma=False)
```

```python
import functools
import math

import jax
import jax.numpy as jnp
from jax import lax
from jax.experimental import pallas as pl
from jax.experimental.pallas import tpu as pltpu
from jax.sharding import PartitionSpec as P

HEADS = 32
SEQS = 2
BLOCK = 256
FORWARD_AFTER = 2
LOG2E = math.log2(math.e)


def softmax_terms(scores, scale):
    scaled = scores * (scale * LOG2E)
    shifted = jnp.exp2(scaled - jnp.max(scaled, axis=0, keepdims=True))
    return shifted, jnp.sum(shifted, axis=0, keepdims=True)


def head_block(teach, stud, stud_t, grad, head, start, tdh, sdh):
    rows = pl.ds(start, BLOCK)
    columns = slice(head * tdh, (head + 1) * tdh)
    dims = (((1,), (1,)), ((), ()))
    stud_own = stud[rows, :]
    lane = lax.broadcasted_iota(jnp.int32, stud_own.shape, 1)
    masked = jnp.where(lane // sdh == head, stud_own, jnp.zeros_like(stud_own))
    teach_scores = lax.dot_general(
        teach[:, columns], teach[rows, columns], dims, preferred_element_type=jnp.float32
    )
    stud_scores = lax.dot_general(stud[...], masked, dims, preferred_element_type=jnp.float32)
    teach_exp, teach_sum = softmax_terms(teach_scores, tdh**-0.5)
    stud_exp, stud_sum = softmax_terms(stud_scores, sdh**-0.5)
    factor = 256.0 * sdh**-0.5
    coef = (stud_exp * (factor / stud_sum) - teach_exp * (factor / teach_sum)).astype(jnp.bfloat16)
    grad[...] += jnp.dot(coef, masked, preferred_element_type=jnp.float32)
    query_side = jnp.dot(stud_t[...], coef, preferred_element_type=jnp.float32)
    sub = lax.broadcasted_iota(jnp.int32, query_side.shape, 0)
    query_side = jnp.where(sub // sdh == head, query_side, 0.0)
    grad[rows, :] += query_side.T


def head_pass(teach, stud, stud_t, grad, head, first, last, tdh, sdh):
    @pl.loop(first, last)
    def _(block):
        head_block(teach, stud, stud_t, grad, head, pl.multiple_of(block * BLOCK, BLOCK), tdh, sdh)


def fused_kernel(
    n_tensor, group_size, tdh, sdh,
    teacher_q, teacher_v, student_q, student_v, out_q, out_v,
    teach, stud, stud_t, grad, result,
    teach_send, teach_recv, teach_local, stud_send, stud_recv, stud_local,
    out_send, out_recv, out_local, fwd_send, fwd_recv,
):
    tensor = lax.axis_index("tensor")
    seq = lax.axis_index("seq")
    member = lax.rem(seq, group_size)
    base = seq - member
    teachers, students, outs = (teacher_q, teacher_v), (student_q, student_v), (out_q, out_v)
    tok = teacher_q.shape[0]
    length = tok * group_size
    pair = 2 * sdh
    blocks = length // BLOCK

    def to(step):
        return lax.rem(member + step, group_size)

    def source(step):
        return lax.rem(member + group_size - step, group_size)

    def t_to(step):
        return lax.rem(tensor + step, n_tensor)

    def t_from(step):
        return lax.rem(tensor + n_tensor - step, n_tensor)

    def rows_of(index):
        return pl.ds(pl.multiple_of(index * tok, tok), tok)

    def teach_copy(rel, head, step, row_owner):
        column = pl.multiple_of((to(step) * 2 + head) * tdh, tdh)
        src = teachers[rel].at[:, pl.ds(column, tdh)]
        dst = teach.at[rel, rows_of(row_owner), pl.ds(head * tdh, tdh)]
        if step == 0:
            return pltpu.make_async_copy(src, dst, teach_local.at[rel, head])
        return pltpu.make_async_remote_copy(
            src_ref=src, dst_ref=dst,
            send_sem=teach_send.at[rel, head, step - 1], recv_sem=teach_recv.at[rel, head, step - 1],
            device_id={"seq": base + to(step)}, device_id_type=pl.DeviceIdType.MESH,
        )

    def stud_copy(rel, step, row_owner):
        column = pl.multiple_of((tensor * group_size + to(step)) * pair, pair)
        src = students[rel].at[:, pl.ds(column, pair)]
        dst = stud.at[rel, rows_of(row_owner), :]
        if step == 0:
            return pltpu.make_async_copy(src, dst, stud_local.at[rel])
        return pltpu.make_async_remote_copy(
            src_ref=src, dst_ref=dst,
            send_sem=stud_send.at[rel, step - 1], recv_sem=stud_recv.at[rel, step - 1],
            device_id={"seq": base + to(step)}, device_id_type=pl.DeviceIdType.MESH,
        )

    def out_copy(rel, step, owner):
        src = result.at[rel, rows_of(to(step)), :]
        column = pl.multiple_of((tensor * group_size + owner) * pair, pair)
        dst = outs[rel].at[:, pl.ds(column, pair)]
        if step == 0:
            return pltpu.make_async_copy(src, dst, out_local.at[rel])
        return pltpu.make_async_remote_copy(
            src_ref=src, dst_ref=dst,
            send_sem=out_send.at[rel, step - 1], recv_sem=out_recv.at[rel, step - 1],
            device_id={"seq": base + to(step)}, device_id_type=pl.DeviceIdType.MESH,
        )

    def fwd_copy(rel, step, owner):
        width = group_size * pair
        columns = pl.ds(pl.multiple_of(owner * width, width), width)
        return pltpu.make_async_remote_copy(
            src_ref=outs[rel].at[:, columns], dst_ref=outs[rel].at[:, columns],
            send_sem=fwd_send.at[rel, step - 1], recv_sem=fwd_recv.at[rel, step - 1],
            device_id={"tensor": t_to(step)}, device_id_type=pl.DeviceIdType.MESH,
        )

    steps = range(1, group_size)
    t_steps = range(1, n_tensor)
    barrier = pltpu.get_barrier_semaphore()
    for step in steps:
        pl.semaphore_signal(
            barrier, inc=1, device_id={"seq": base + to(step)}, device_id_type=pl.DeviceIdType.MESH
        )
    for step in t_steps:
        pl.semaphore_signal(
            barrier, inc=1, device_id={"tensor": t_to(step)}, device_id_type=pl.DeviceIdType.MESH
        )

    stud_copy(0, 0, member).start()
    teach_copy(0, 0, 0, member).start()
    pl.semaphore_wait(barrier, group_size - 1 + n_tensor - 1)

    def start_stud(rel):
        for step in steps:
            stud_copy(rel, step, member).start()

    def start_teach(rel, head):
        for step in steps:
            teach_copy(rel, head, step, member).start()

    def finish_stud(rel):
        stud_copy(rel, 0, member).wait()
        for step in steps:
            stud_copy(rel, step, source(step)).wait_recv()

    def finish_teach(rel, head):
        teach_copy(rel, head, 0, member).wait()
        for step in steps:
            teach_copy(rel, head, step, source(step)).wait_recv()

    def start_out(rel):
        out_copy(rel, 0, member).start()
        for step in steps:
            out_copy(rel, step, member).start()

    def forward(rel):
        out_copy(rel, 0, member).wait()
        for step in steps:
            out_copy(rel, step, source(step)).wait_recv()
        for step in t_steps:
            fwd_copy(rel, step, tensor).start()

    start_stud(0)
    start_teach(0, 0)
    start_teach(0, 1)
    for rel, head in ((0, 1), (1, 0), (1, 1)):
        teach_copy(rel, head, 0, member).start()
    stud_copy(1, 0, member).start()

    for rel in range(2):
        finish_stud(rel)
        finish_teach(rel, 0)
        if rel == 0:
            start_stud(1)
            start_teach(1, 0)
        stud_t[...] = stud[rel].T
        grad[...] = jnp.zeros_like(grad)
        args = (teach.at[rel], stud.at[rel], stud_t, grad)
        if rel == 1:
            head_pass(*args, 0, 0, FORWARD_AFTER, tdh, sdh)
            forward(0)
            head_pass(*args, 0, FORWARD_AFTER, blocks, tdh, sdh)
        else:
            head_pass(*args, 0, 0, blocks, tdh, sdh)
        finish_teach(rel, 1)
        if rel == 0:
            start_teach(1, 1)
        head_pass(*args, 1, 0, blocks, tdh, sdh)
        result[rel] = grad[...].astype(result.dtype)
        start_out(rel)
    forward(1)

    for rel in range(2):
        for step in t_steps:
            fwd_copy(rel, step, t_from(step)).wait_recv()
        for step in steps:
            stud_copy(rel, step, member).wait_send()
            teach_copy(rel, 0, step, member).wait_send()
            teach_copy(rel, 1, step, member).wait_send()
            out_copy(rel, step, member).wait_send()
        for step in t_steps:
            fwd_copy(rel, step, tensor).wait_send()


def shards_pairs(teacher_q, teacher_v, student_q, student_v):
    n_tensor = lax.axis_size("tensor")
    group_size = lax.axis_size("seq") // SEQS
    tdh = teacher_q.shape[1] * n_tensor // HEADS
    sdh = student_q.shape[1] // HEADS
    length = teacher_q.shape[0] * group_size
    pair = 2 * sdh
    dma = pltpu.SemaphoreType.DMA
    out = jax.ShapeDtypeStruct(student_q.shape, student_q.dtype)
    return pl.pallas_call(
        functools.partial(fused_kernel, n_tensor, group_size, tdh, sdh),
        out_shape=(out, out),
        in_specs=[pl.BlockSpec(memory_space=pl.ANY)] * 4,
        out_specs=(pl.BlockSpec(memory_space=pl.ANY),) * 2,
        scratch_shapes=[
            pltpu.VMEM((2, length, 2 * tdh), jnp.bfloat16),
            pltpu.VMEM((2, length, pair), jnp.bfloat16),
            pltpu.VMEM((pair, length), jnp.bfloat16),
            pltpu.VMEM((length, pair), jnp.float32),
            pltpu.VMEM((2, length, pair), jnp.bfloat16),
            dma((2, 2, group_size - 1)),
            dma((2, 2, group_size - 1)),
            dma((2, 2)),
            dma((2, group_size - 1)),
            dma((2, group_size - 1)),
            dma((2,)),
            dma((2, group_size - 1)),
            dma((2, group_size - 1)),
            dma((2,)),
            dma((2, n_tensor - 1)),
            dma((2, n_tensor - 1)),
        ],
        compiler_params=pltpu.CompilerParams(
            collective_id=0, has_side_effects=True, vmem_limit_bytes=56 * 2**20
        ),
    )(teacher_q, teacher_v, student_q, student_v)


def from_partner(array, axis, distance):
    return lax.ppermute(array, axis, [(i, i ^ 1 << distance) for i in range(lax.axis_size(axis))])


def head_terms(teach_query, teach_key, stud_query, stud_key, teach_dim, stud_dim):
    teach_scores = jnp.dot(
        teach_query, teach_key.T, preferred_element_type=jnp.float32
    ) * teach_dim ** (-0.5)
    stud_scores = jnp.dot(
        stud_query, stud_key.T, preferred_element_type=jnp.float32
    ) * stud_dim ** (-0.5)
    teach_prob = jax.nn.softmax(teach_scores, axis=-1)
    stud_prob = jax.nn.softmax(stud_scores, axis=-1)
    coef = (256.0 * stud_dim ** (-0.5) * (stud_prob - teach_prob)).astype(jnp.bfloat16)
    query_grad = jnp.dot(coef, stud_key, preferred_element_type=jnp.float32)
    key_grad = jnp.einsum("qk,qd->kd", coef, stud_query, preferred_element_type=jnp.float32)
    return (query_grad, key_grad)


def relate(teach_own, teach_keys, stud_own, stud_keys, per_dev, teach_dim, stud_dim):
    tok_rows = teach_own.shape[0]
    teach_query = teach_own.reshape(tok_rows, per_dev, teach_dim).transpose(1, 0, 2)
    teach_key = teach_keys.reshape(-1, per_dev, teach_dim).transpose(1, 0, 2)
    stud_query = stud_own.reshape(tok_rows, per_dev, stud_dim).transpose(1, 0, 2)
    stud_key = stud_keys.reshape(-1, per_dev, stud_dim).transpose(1, 0, 2)

    def one_head(group):
        return head_terms(group[0], group[1], group[2], group[3], teach_dim, stud_dim)

    query_grad, key_grad = lax.map(one_head, (teach_query, teach_key, stud_query, stud_key))
    return (
        query_grad.transpose(1, 0, 2).reshape(tok_rows, per_dev * stud_dim),
        key_grad.transpose(1, 0, 2).reshape(-1, per_dev * stud_dim),
    )


def shards(teacher_q, teacher_v, student_q, student_v):
    n_tensor = lax.axis_size("tensor")
    n_seq = lax.axis_size("seq")
    per_dev = HEADS // n_tensor
    group_size = n_seq // SEQS
    level_count = group_size.bit_length() - 1
    seq_index = lax.axis_index("seq")
    member = seq_index % group_size
    teach_dim = teacher_q.shape[1] // per_dev
    stud_dim = student_q.shape[1] // HEADS
    own_width = per_dev * stud_dim
    offset = lax.axis_index("tensor") * own_width
    own_q = lax.dynamic_slice_in_dim(student_q, offset, own_width, 1)
    own_v = lax.dynamic_slice_in_dim(student_v, offset, own_width, 1)
    key_tq, key_tv, key_sq, key_sv = (teacher_q, teacher_v, own_q, own_v)
    for bit_num in range(level_count):
        partner = from_partner((key_tq, key_tv, key_sq, key_sv), "seq", bit_num)
        upper_half = member // 2**bit_num % 2 == 1
        joined = []
        for mine, theirs in zip((key_tq, key_tv, key_sq, key_sv), partner):
            joined.append(
                jnp.where(
                    upper_half,
                    jnp.concatenate([theirs, mine], 0),
                    jnp.concatenate([mine, theirs], 0),
                )
            )
        key_tq, key_tv, key_sq, key_sv = joined
    q_query, q_key = relate(teacher_q, key_tq, own_q, key_sq, per_dev, teach_dim, stud_dim)
    v_query, v_key = relate(teacher_v, key_tv, own_v, key_sv, per_dev, teach_dim, stud_dim)
    returned = jnp.concatenate([q_key, v_key], axis=1)
    for bit_num in reversed(range(level_count)):
        half_rows = returned.shape[0] // 2
        upper_half = member // 2**bit_num % 2 == 1
        low_part = returned[:half_rows]
        high_part = returned[half_rows:]
        kept = jnp.where(upper_half, high_part, low_part)
        outgoing = jnp.where(upper_half, low_part, high_part)
        returned = kept + from_partner(outgoing.astype(jnp.bfloat16), "seq", bit_num).astype(
            outgoing.dtype
        )
    head_q = (q_query + returned[:, :own_width]).astype(jnp.bfloat16)
    head_v = (v_query + returned[:, own_width:]).astype(jnp.bfloat16)
    full_q, full_v = (
        lax.all_gather(head_q, "tensor", axis=1, tiled=True),
        lax.all_gather(head_v, "tensor", axis=1, tiled=True),
    )
    return (full_q, full_v)


def solution(mesh):
    per_dev = HEADS // mesh.shape["tensor"]
    group_size = mesh.shape["seq"] // SEQS
    body = shards_pairs if per_dev == 2 * group_size else shards
    in_specs = (P("seq", "tensor"), P("seq", "tensor"), P("seq", None), P("seq", None))
    out_specs = (P("seq", None), P("seq", None))
    return jax.shard_map(body, mesh=mesh, in_specs=in_specs, out_specs=out_specs, check_vma=False)
```

```python
import functools
import math

import jax
import jax.numpy as jnp
from jax import lax
from jax.experimental import pallas as pl
from jax.experimental.pallas import tpu as pltpu
from jax.sharding import PartitionSpec as P

HEADS = 32
SEQS = 2
BLOCK = 256
CHUNK = 128
PRODUCT = 256
RELAYS = (((2, 0), (6, 1)), ((3, 2),))
LOG2E = math.log2(math.e)


def prepare_head(stud, stud_t, masked, head, sdh):
    lane = lax.broadcasted_iota(jnp.int32, stud.shape, 1)
    masked[...] = jnp.where(lane // sdh == head, stud[...], jnp.zeros(stud.shape, stud.dtype))
    stud_t[...] = masked[...].T


def add_chunk(k, scores, scale, exps, tops, top, total):
    size = scores.shape[0]
    scores = scores.reshape(size // 8, 8, BLOCK) * (scale * LOG2E)
    new_top = jnp.max(scores, axis=0)
    if k:
        new_top = jnp.maximum(top, new_top)
    shifted = jnp.exp2(scores - new_top[None])
    part = jnp.sum(shifted, axis=0)
    new_total = total * jnp.exp2(top - new_top) + part if k else part
    exps[k * size : (k + 1) * size, :] = shifted.reshape(size, BLOCK)
    tops[k * 8 : (k + 1) * 8, :] = new_top
    return new_top, new_total


def finish_softmax(top, total, factor):
    all_top = jnp.max(top, axis=0, keepdims=True)
    return all_top, factor / jnp.sum(total * jnp.exp2(top - all_top), axis=0, keepdims=True)


def head_pass(refs, head, first, last, tdh, sdh):
    teach, stud, stud_t, masked, grad, teach_exps, stud_exps, teach_tops, stud_tops = refs
    dims = (((1,), (1,)), ((), ()))
    length = stud.shape[0]
    columns = slice(head * tdh, (head + 1) * tdh)
    factor = 256.0 * sdh**-0.5

    @pl.loop(first, last)
    def _(block):
        rows = pl.ds(pl.multiple_of(block * BLOCK, BLOCK), BLOCK)
        teach_own = teach[rows, columns]
        stud_own = masked[rows, :]
        t_top = t_total = s_top = s_total = None
        for k in range(length // CHUNK):
            keys = slice(k * CHUNK, (k + 1) * CHUNK)
            teach_scores = lax.dot_general(
                teach[keys, columns], teach_own, dims, preferred_element_type=jnp.float32
            )
            stud_scores = lax.dot_general(
                stud[keys, :], stud_own, dims, preferred_element_type=jnp.float32
            )
            t_top, t_total = add_chunk(k, teach_scores, tdh**-0.5, teach_exps, teach_tops, t_top, t_total)
            s_top, s_total = add_chunk(k, stud_scores, sdh**-0.5, stud_exps, stud_tops, s_top, s_total)
        t_top, t_factor = finish_softmax(t_top, t_total, factor)
        s_top, s_factor = finish_softmax(s_top, s_total, factor)
        query_side = None
        for k in range(length // PRODUCT):
            parts = []
            for c in range(k * PRODUCT // CHUNK, (k + 1) * PRODUCT // CHUNK):
                keys, top_rows = slice(c * CHUNK, (c + 1) * CHUNK), slice(c * 8, (c + 1) * 8)
                t_mul = jnp.exp2(teach_tops[top_rows, :] - t_top) * t_factor
                s_mul = jnp.exp2(stud_tops[top_rows, :] - s_top) * s_factor
                coef = (
                    stud_exps[keys, :].reshape(CHUNK // 8, 8, BLOCK) * s_mul[None]
                    - teach_exps[keys, :].reshape(CHUNK // 8, 8, BLOCK) * t_mul[None]
                )
                parts.append(coef.reshape(CHUNK, BLOCK).astype(jnp.bfloat16))
            coef = jnp.concatenate(parts, axis=0)
            keys = slice(k * PRODUCT, (k + 1) * PRODUCT)
            grad[keys, :] += jnp.dot(coef, stud_own, preferred_element_type=jnp.float32)
            part = jnp.dot(stud_t[:, keys], coef, preferred_element_type=jnp.float32)
            query_side = part if query_side is None else query_side + part
        grad[rows, :] += query_side.T


def fused_kernel(
    n_tensor, group_size, tdh, sdh,
    teacher_q, teacher_v, student_q, student_v, out_q, out_v,
    teach, stud, stud_t, masked, grad, teach_exps, stud_exps, teach_tops, stud_tops, result,
    teach_send, teach_recv, teach_local, stud_send, stud_recv, stud_local,
    out_send, out_recv, out_local, fwd_send, fwd_recv,
):
    tensor = lax.axis_index("tensor")
    seq = lax.axis_index("seq")
    member = lax.rem(seq, group_size)
    base = seq - member
    teachers, students, outs = (teacher_q, teacher_v), (student_q, student_v), (out_q, out_v)
    tok = teacher_q.shape[0]
    length = tok * group_size
    pair = 2 * sdh
    blocks = length // BLOCK

    def to(step):
        return lax.rem(member + step, group_size)

    def source(step):
        return lax.rem(member + group_size - step, group_size)

    def rows_of(index):
        return pl.ds(pl.multiple_of(index * tok, tok), tok)

    def teach_copy(rel, head, step, row_owner):
        column = pl.multiple_of((to(step) * 2 + head) * tdh, tdh)
        src = teachers[rel].at[:, pl.ds(column, tdh)]
        dst = teach.at[rel, rows_of(row_owner), pl.ds(head * tdh, tdh)]
        if step == 0:
            return pltpu.make_async_copy(src, dst, teach_local.at[rel, head])
        return pltpu.make_async_remote_copy(
            src_ref=src, dst_ref=dst,
            send_sem=teach_send.at[rel, head, step - 1], recv_sem=teach_recv.at[rel, head, step - 1],
            device_id={"seq": base + to(step)}, device_id_type=pl.DeviceIdType.MESH,
        )

    def stud_copy(rel, step, row_owner):
        column = pl.multiple_of((tensor * group_size + to(step)) * pair, pair)
        src = students[rel].at[:, pl.ds(column, pair)]
        dst = stud.at[rel, rows_of(row_owner), :]
        if step == 0:
            return pltpu.make_async_copy(src, dst, stud_local.at[rel])
        return pltpu.make_async_remote_copy(
            src_ref=src, dst_ref=dst,
            send_sem=stud_send.at[rel, step - 1], recv_sem=stud_recv.at[rel, step - 1],
            device_id={"seq": base + to(step)}, device_id_type=pl.DeviceIdType.MESH,
        )

    def out_copy(rel, step, owner):
        src = result.at[rel, rows_of(to(step)), :]
        column = pl.multiple_of((tensor * group_size + owner) * pair, pair)
        dst = outs[rel].at[:, pl.ds(column, pair)]
        if step == 0:
            return pltpu.make_async_copy(src, dst, out_local.at[rel])
        return pltpu.make_async_remote_copy(
            src_ref=src, dst_ref=dst,
            send_sem=out_send.at[rel, step - 1], recv_sem=out_recv.at[rel, step - 1],
            device_id={"seq": base + to(step)}, device_id_type=pl.DeviceIdType.MESH,
        )

    def relay_copy(rel, step, way, chunk):
        origin = tensor - step if way == 0 else tensor + step
        column = pl.multiple_of((origin * group_size + source(chunk)) * pair, pair)
        block = outs[rel].at[:, pl.ds(column, pair)]
        return pltpu.make_async_remote_copy(
            src_ref=block, dst_ref=block,
            send_sem=fwd_send.at[rel, way, step, chunk], recv_sem=fwd_recv.at[rel, way, step, chunk],
            device_id={"tensor": tensor + 1 if way == 0 else tensor - 1},
            device_id_type=pl.DeviceIdType.MESH,
        )

    def has_origin(step, way):
        return tensor >= step if way == 0 else tensor + step < n_tensor

    def has_next(way):
        return tensor + 1 < n_tensor if way == 0 else tensor > 0

    def arrived(rel, step, way, chunk):
        origin = tensor - step if way == 0 else tensor + step
        column = pl.multiple_of((origin * group_size + source(chunk)) * pair, pair)
        block = outs[rel].at[:, pl.ds(column, pair)]
        pltpu.make_async_remote_copy(
            src_ref=block, dst_ref=block,
            send_sem=fwd_send.at[rel, way, step - 1, chunk], recv_sem=fwd_recv.at[rel, way, step - 1, chunk],
            device_id={"tensor": tensor + 1 if way == 0 else tensor - 1},
            device_id_type=pl.DeviceIdType.MESH,
        ).wait_recv()

    def relay(rel, step):
        for chunk in range(group_size):
            if step == 0:
                if chunk == 0:
                    out_copy(rel, 0, member).wait()
                else:
                    out_copy(rel, chunk, source(chunk)).wait_recv()
            for way in range(2):
                if step:
                    @pl.when(has_origin(step, way))
                    def _():
                        arrived(rel, step, way, chunk)

                if step < n_tensor - 1:
                    @pl.when(has_origin(step, way) & has_next(way))
                    def _():
                        relay_copy(rel, step, way, chunk).start()

    def relay_sent(rel):
        for step in range(n_tensor - 1):
            for way in range(2):
                @pl.when(has_origin(step, way) & has_next(way))
                def _():
                    for chunk in range(group_size):
                        relay_copy(rel, step, way, chunk).wait_send()

    steps = range(1, group_size)
    barrier = pltpu.get_barrier_semaphore()
    for step in steps:
        pl.semaphore_signal(
            barrier, inc=1, device_id={"seq": base + to(step)}, device_id_type=pl.DeviceIdType.MESH
        )
    for step in range(1, n_tensor):
        pl.semaphore_signal(
            barrier, inc=1, device_id={"tensor": lax.rem(tensor + step, n_tensor)},
            device_id_type=pl.DeviceIdType.MESH,
        )

    stud_copy(0, 0, member).start()
    teach_copy(0, 0, 0, member).start()
    pl.semaphore_wait(barrier, group_size - 1 + n_tensor - 1)

    def start_stud(rel):
        for step in steps:
            stud_copy(rel, step, member).start()

    def start_teach(rel, head):
        for step in steps:
            teach_copy(rel, head, step, member).start()

    def finish_stud(rel):
        stud_copy(rel, 0, member).wait()
        for step in steps:
            stud_copy(rel, step, source(step)).wait_recv()

    def finish_teach(rel, head):
        teach_copy(rel, head, 0, member).wait()
        for step in steps:
            teach_copy(rel, head, step, source(step)).wait_recv()

    def start_out(rel):
        out_copy(rel, 0, member).start()
        for step in steps:
            out_copy(rel, step, member).start()

    start_stud(0)
    start_teach(0, 0)
    start_teach(0, 1)
    for rel, head in ((0, 1), (1, 0), (1, 1)):
        teach_copy(rel, head, 0, member).start()
    stud_copy(1, 0, member).start()

    for rel in range(2):
        finish_stud(rel)
        finish_teach(rel, 0)
        if rel == 0:
            start_stud(1)
            start_teach(1, 0)
        grad[...] = jnp.zeros_like(grad)
        refs = (
            teach.at[rel], stud.at[rel], stud_t, masked, grad,
            teach_exps, stud_exps, teach_tops, stud_tops,
        )
        for head in range(2):
            if head:
                finish_teach(rel, 1)
                if rel == 0:
                    start_teach(1, 1)
            prepare_head(*refs[1:4], head, sdh)
            first = 0
            if rel:
                for at, step in RELAYS[head]:
                    head_pass(refs, head, first, blocks * at // 8, tdh, sdh)
                    relay(0, step)
                    first = blocks * at // 8
            head_pass(refs, head, first, blocks, tdh, sdh)
        result[rel] = grad[...].astype(result.dtype)
        start_out(rel)
    relay(0, n_tensor - 1)
    for step in range(n_tensor):
        relay(1, step)

    for rel in range(2):
        for step in steps:
            stud_copy(rel, step, member).wait_send()
            teach_copy(rel, 0, step, member).wait_send()
            teach_copy(rel, 1, step, member).wait_send()
            out_copy(rel, step, member).wait_send()
        relay_sent(rel)


def shards_pairs(teacher_q, teacher_v, student_q, student_v):
    n_tensor = lax.axis_size("tensor")
    group_size = lax.axis_size("seq") // SEQS
    tdh = teacher_q.shape[1] * n_tensor // HEADS
    sdh = student_q.shape[1] // HEADS
    length = teacher_q.shape[0] * group_size
    pair = 2 * sdh
    dma = pltpu.SemaphoreType.DMA
    out = jax.ShapeDtypeStruct(student_q.shape, student_q.dtype)
    return pl.pallas_call(
        functools.partial(fused_kernel, n_tensor, group_size, tdh, sdh),
        out_shape=(out, out),
        in_specs=[pl.BlockSpec(memory_space=pl.ANY)] * 4,
        out_specs=(pl.BlockSpec(memory_space=pl.ANY),) * 2,
        scratch_shapes=[
            pltpu.VMEM((2, length, 2 * tdh), jnp.bfloat16),
            pltpu.VMEM((2, length, pair), jnp.bfloat16),
            pltpu.VMEM((pair, length), jnp.bfloat16),
            pltpu.VMEM((length, pair), jnp.bfloat16),
            pltpu.VMEM((length, pair), jnp.float32),
            pltpu.VMEM((length, BLOCK), jnp.float32),
            pltpu.VMEM((length, BLOCK), jnp.float32),
            pltpu.VMEM((length // CHUNK * 8, BLOCK), jnp.float32),
            pltpu.VMEM((length // CHUNK * 8, BLOCK), jnp.float32),
            pltpu.VMEM((2, length, pair), jnp.bfloat16),
            dma((2, 2, group_size - 1)),
            dma((2, 2, group_size - 1)),
            dma((2, 2)),
            dma((2, group_size - 1)),
            dma((2, group_size - 1)),
            dma((2,)),
            dma((2, group_size - 1)),
            dma((2, group_size - 1)),
            dma((2,)),
            dma((2, 2, n_tensor - 1, group_size)),
            dma((2, 2, n_tensor - 1, group_size)),
        ],
        compiler_params=pltpu.CompilerParams(
            collective_id=0, has_side_effects=True, vmem_limit_bytes=56 * 2**20
        ),
    )(teacher_q, teacher_v, student_q, student_v)


def from_partner(array, axis, distance):
    return lax.ppermute(array, axis, [(i, i ^ 1 << distance) for i in range(lax.axis_size(axis))])


def head_terms(teach_query, teach_key, stud_query, stud_key, teach_dim, stud_dim):
    teach_scores = jnp.dot(
        teach_query, teach_key.T, preferred_element_type=jnp.float32
    ) * teach_dim ** (-0.5)
    stud_scores = jnp.dot(
        stud_query, stud_key.T, preferred_element_type=jnp.float32
    ) * stud_dim ** (-0.5)
    teach_prob = jax.nn.softmax(teach_scores, axis=-1)
    stud_prob = jax.nn.softmax(stud_scores, axis=-1)
    coef = (256.0 * stud_dim ** (-0.5) * (stud_prob - teach_prob)).astype(jnp.bfloat16)
    query_grad = jnp.dot(coef, stud_key, preferred_element_type=jnp.float32)
    key_grad = jnp.einsum("qk,qd->kd", coef, stud_query, preferred_element_type=jnp.float32)
    return (query_grad, key_grad)


def relate(teach_own, teach_keys, stud_own, stud_keys, per_dev, teach_dim, stud_dim):
    tok_rows = teach_own.shape[0]
    teach_query = teach_own.reshape(tok_rows, per_dev, teach_dim).transpose(1, 0, 2)
    teach_key = teach_keys.reshape(-1, per_dev, teach_dim).transpose(1, 0, 2)
    stud_query = stud_own.reshape(tok_rows, per_dev, stud_dim).transpose(1, 0, 2)
    stud_key = stud_keys.reshape(-1, per_dev, stud_dim).transpose(1, 0, 2)

    def one_head(group):
        return head_terms(group[0], group[1], group[2], group[3], teach_dim, stud_dim)

    query_grad, key_grad = lax.map(one_head, (teach_query, teach_key, stud_query, stud_key))
    return (
        query_grad.transpose(1, 0, 2).reshape(tok_rows, per_dev * stud_dim),
        key_grad.transpose(1, 0, 2).reshape(-1, per_dev * stud_dim),
    )


def shards(teacher_q, teacher_v, student_q, student_v):
    n_tensor = lax.axis_size("tensor")
    n_seq = lax.axis_size("seq")
    per_dev = HEADS // n_tensor
    group_size = n_seq // SEQS
    level_count = group_size.bit_length() - 1
    seq_index = lax.axis_index("seq")
    member = seq_index % group_size
    teach_dim = teacher_q.shape[1] // per_dev
    stud_dim = student_q.shape[1] // HEADS
    own_width = per_dev * stud_dim
    offset = lax.axis_index("tensor") * own_width
    own_q = lax.dynamic_slice_in_dim(student_q, offset, own_width, 1)
    own_v = lax.dynamic_slice_in_dim(student_v, offset, own_width, 1)
    key_tq, key_tv, key_sq, key_sv = (teacher_q, teacher_v, own_q, own_v)
    for bit_num in range(level_count):
        partner = from_partner((key_tq, key_tv, key_sq, key_sv), "seq", bit_num)
        upper_half = member // 2**bit_num % 2 == 1
        joined = []
        for mine, theirs in zip((key_tq, key_tv, key_sq, key_sv), partner):
            joined.append(
                jnp.where(
                    upper_half,
                    jnp.concatenate([theirs, mine], 0),
                    jnp.concatenate([mine, theirs], 0),
                )
            )
        key_tq, key_tv, key_sq, key_sv = joined
    q_query, q_key = relate(teacher_q, key_tq, own_q, key_sq, per_dev, teach_dim, stud_dim)
    v_query, v_key = relate(teacher_v, key_tv, own_v, key_sv, per_dev, teach_dim, stud_dim)
    returned = jnp.concatenate([q_key, v_key], axis=1)
    for bit_num in reversed(range(level_count)):
        half_rows = returned.shape[0] // 2
        upper_half = member // 2**bit_num % 2 == 1
        low_part = returned[:half_rows]
        high_part = returned[half_rows:]
        kept = jnp.where(upper_half, high_part, low_part)
        outgoing = jnp.where(upper_half, low_part, high_part)
        returned = kept + from_partner(outgoing.astype(jnp.bfloat16), "seq", bit_num).astype(
            outgoing.dtype
        )
    head_q = (q_query + returned[:, :own_width]).astype(jnp.bfloat16)
    head_v = (v_query + returned[:, own_width:]).astype(jnp.bfloat16)
    full_q, full_v = (
        lax.all_gather(head_q, "tensor", axis=1, tiled=True),
        lax.all_gather(head_v, "tensor", axis=1, tiled=True),
    )
    return (full_q, full_v)


def solution(mesh):
    per_dev = HEADS // mesh.shape["tensor"]
    group_size = mesh.shape["seq"] // SEQS
    body = shards_pairs if per_dev == 2 * group_size and mesh.shape["tensor"] == 4 else shards
    in_specs = (P("seq", "tensor"), P("seq", "tensor"), P("seq", None), P("seq", None))
    out_specs = (P("seq", None), P("seq", None))
    return jax.shard_map(body, mesh=mesh, in_specs=in_specs, out_specs=out_specs, check_vma=False)
```
